32 devices in a mesh: row: 4 (over y, x), col: 8 (over z, core).
Axes of the slice: x: 2, y: 2, z: 4, core: 2. Of those that a mesh axis runs over, the one named last changes fastest.
Arguments:
- snapshots: float32 [4, 256, 1024], P('row', 'col'), may hold values from -6 to 6
- operator: float32 [65536, 1024], P('row', 'col'), may hold values from -0.1875 to 0.1875
Outputs:
- reduced: float32 [4, 256, 65536], P(None, 'col', 'row')
The draws below stay inside these ranges and needn't reach their ends.
All inputs are finite; a program needn't handle non-finite values.
Results may differ from the reference program's by a relative error of at most 0.00007.
Values sent between devices are 32-bit elements; how exact they have to be, the bound alone decides.
No kernel may reach another device: no remote copies, remote signals or barrier semaphores. Data moves between devices by JAX's collectives and lax.ppermute only.
A program may use at most 192 MiB of HBM per device.

```python
import jax
import jax.numpy as jnp
from jax import lax

MODES = 65536
VIS = 1024
GROUPS = 4
TPER = 256


def steps_of(rng, shape, cuts, low, high):
    def one(dim, shards_of):
        draws = jax.random.uniform(jax.random.fold_in(jax.random.fold_in(rng, 6), dim), (shards_of,), jnp.float32, low / len(cuts), high / len(cuts))
        return jnp.repeat(jnp.exp(draws), shape[dim] // shards_of).reshape((-1,) + (1,) * (len(shape) - dim - 1))

    gain = one(*cuts[0])
    for cut in cuts[1:]:
        gain = gain * one(*cut)
    return gain


def scatter_about(rng, shape, spread, most, cuts=(), kind=jnp.bfloat16):
    loudness = steps_of(rng, shape, cuts, -0.22, 0.18) if cuts else 1.0
    array = jax.random.normal(rng, shape, jnp.float32) * spread * loudness
    return jnp.minimum(jnp.maximum(array, -most), most).astype(kind)


def setup_inputs(seed: int = 0) -> dict:
    keys = jax.random.split(jax.random.key(seed), 3)
    snapshots = scatter_about(keys[0], (GROUPS, TPER, VIS), 1.0, 6.0, ((0, 4), (1, 8)), jnp.float32)
    operator = scatter_about(keys[1], (MODES, VIS), VIS ** -0.5, 0.1875, ((0, 4), (1, 8)), jnp.float32)
    return dict(snapshots=snapshots, operator=operator)


def reference(snapshots, operator):
    groups, times, width = snapshots.shape
    flat_rows = snapshots.reshape(groups * times, width)
    result = lax.dot_general(flat_rows, operator, (((1,), (1,)), ((), ())), precision=lax.Precision.HIGHEST, preferred_element_type=jnp.float32)
    return result.reshape(groups, times, operator.shape[0])
```

```python
import functools

import jax
import jax.numpy as jnp
from jax import lax
from jax.experimental import pallas as pl
from jax.experimental.pallas import tpu as pltpu
from jax.sharding import PartitionSpec as P

CORES = 2
PARTS = 4
BLOCK = 512


def split(x):
    high = x.astype(jnp.bfloat16)
    low = (x - high.astype(jnp.float32)).astype(jnp.bfloat16)
    return high, low


def dot(left, right):
    return lax.dot_general(
        left, right, (((1,), (1,)), ((), ())), preferred_element_type=jnp.float32
    )


def product_kernel(rows_ref, *refs):
    pieces, out_ref, high_ref, low_ref = refs[:-3], refs[-3], refs[-2], refs[-1]

    @pl.when(pl.program_id(0) == 0)
    def _():
        high, low = split(rows_ref[...])
        high_ref[...] = high
        low_ref[...] = low

    modes = [piece[...] for piece in pieces]
    high, low = split(modes[0] if len(modes) == 1 else jnp.concatenate(modes, axis=1))
    row_high = high_ref[...]
    out_ref[...] = dot(row_high, high) + (dot(row_high, low) + dot(low_ref[...], high))


def product(rows, pieces):
    if pieces[0].shape[1] % 128:
        pieces = [jnp.concatenate(pieces, axis=1)]
    height, depth = rows.shape
    modes = pieces[0].shape[0]
    block = min(BLOCK, modes)
    return pl.pallas_call(
        product_kernel,
        grid=(modes // block,),
        in_specs=[pl.BlockSpec((height, depth), lambda i: (0, 0))]
        + [pl.BlockSpec((block, piece.shape[1]), lambda i: (i, 0)) for piece in pieces],
        out_specs=pl.BlockSpec((height, block), lambda i: (0, i)),
        out_shape=jax.ShapeDtypeStruct((height, modes), jnp.float32),
        scratch_shapes=[pltpu.VMEM((height, depth), jnp.bfloat16)] * 2,
        compiler_params=pltpu.CompilerParams(vmem_limit_bytes=48 * 2**20),
        cost_estimate=pl.CostEstimate(
            flops=6 * height * depth * modes,
            bytes_accessed=4 * (height * depth + depth * modes + height * modes),
            transcendentals=0,
        ),
    )(rows, *pieces)


def shards(snapshots, operator):
    chips = lax.axis_size("col") // CORES
    half = chips // 2
    modes, width = operator.shape
    col = lax.axis_index("col")
    chip, core = col // CORES, col % CORES
    side = (chip >= half).astype(jnp.int32)
    place = jnp.where(side == 0, half - 1 - chip, chip - half)

    def at(side, place):
        return (half - 1 - place) + side * (2 * place + 1)

    def move(x, routes):
        pairs = [
            (at(a, i) * CORES + c, at(b, j) * CORES + c)
            for (a, i), (b, j) in routes
            for c in range(CORES)
        ]
        return lax.ppermute(x, "col", pairs)

    def inward(x, i):
        return move(x, [((s, i), (s, 0)) for s in range(2)])

    def outward(x, i):
        return move(x, [((s, 0), (s, i)) for s in range(2)])

    def across(x, i=0):
        return move(x, [((s, 0), (1 - s, i)) for s in range(2)])

    def turn(x, i):
        return move(x, [((s, j), (s, (j + i) % half)) for s in range(2) for j in range(half)])

    def swap(x):
        pairs = [(q * CORES + c, q * CORES + 1 - c) for q in range(chips) for c in range(CORES)]
        return lax.ppermute(x, "col", pairs)

    times = snapshots.shape[1]
    flat = lax.all_gather(snapshots, "col", axis=1, tiled=True)
    flat = lax.all_gather(flat, "row", axis=0, tiled=True)
    groups = flat.shape[0]
    height = groups * times

    def rows_of(chip, core):
        block = lax.dynamic_slice_in_dim(flat, (chip * CORES + core) * times, times, axis=1)
        return block.reshape(height, flat.shape[2])

    def columns_of(rows, chip):
        return lax.dynamic_slice_in_dim(rows, (chip * CORES + core) * width, width, axis=1)

    def left_side(row_chips, column_chips):
        rows = jnp.concatenate([rows_of(q, e) for e in (core, 1 - core) for q in row_chips], axis=0)
        return [columns_of(rows, q) for q in column_chips]

    mine = [at(side, (place + i) % half) for i in range(half)]
    others = [at(1 - side, i) for i in range(half)]
    rows_a = left_side(mine, mine + others)
    for i in range(1, half):
        own = (jnp.arange(CORES * half * height) // height) % half == i
        rows_a[i] = jnp.where(own[:, None], 0.0, rows_a[i])
    rows_a = jnp.concatenate(rows_a, axis=1)
    rows_b = left_side(
        [mine[0]] + others, [at(side, (place - i + half) % half) for i in range(half)]
    )
    rows_b = jnp.concatenate(rows_b, axis=1)

    part = modes // PARTS
    count = PARTS - 1
    last = modes - count * part
    chunk = [operator[k * part : (k + 1) * part] for k in range(count)]
    tail = operator[count * part :]

    hub = across(operator[: count * part])
    inner = [[inward(chunk[k], i) for i in range(1, half)] for k in range(count)]
    pieces_b = [tail] + [turn(tail, i) for i in range(1, half)]
    outer = [[across(x) for x in inner[k]] for k in range(count)]

    sums_b = product(rows_b, pieces_b)
    sums_b = sums_b.reshape(CORES, 1 + half, height, last)
    sums_b = sums_b[0] + swap(sums_b[1])
    total_b = sums_b[0]

    out = jnp.zeros((height, modes), jnp.float32)
    for k in range(count):
        pieces = [chunk[k]] + inner[k] + [hub[k * part : (k + 1) * part]] + outer[k]
        sums = product(rows_a, pieces).reshape(CORES, half, height, part)
        sums = sums[0] + swap(sums[1])
        total = sums[0]
        for i in range(1, half):
            total = total + outward(sums[i], i)
        out = lax.dynamic_update_slice(out, total, (0, k * part))

    for i in reversed(range(half)):
        total_b = total_b + across(sums_b[1 + i], i)
    out = lax.dynamic_update_slice(out, total_b, (0, count * part))
    return out.reshape(groups, times, modes)


def solution(mesh):
    placed = (P("row", "col", None), P("row", "col"))
    return jax.shard_map(
        shards, mesh=mesh, in_specs=placed, out_specs=P(None, "col", "row"), check_vma=False
    )
```

```python
import math

import jax
import jax.numpy as jnp
from jax import lax
from jax.experimental import pallas as pl
from jax.experimental.pallas import tpu as pltpu
from jax.sharding import PartitionSpec as P

CORES = 2
BLOCK = 512
SIXTEENTHS = (4, 4, 4, 4)


def after(x, *others):
    return lax.optimization_barrier((x, *others))[0]


def split(x):
    high = x.astype(jnp.bfloat16)
    low = (x - high.astype(jnp.float32)).astype(jnp.bfloat16)
    return high, low


def dot(left, right):
    return lax.dot_general(
        left, right, (((1,), (1,)), ((), ())), preferred_element_type=jnp.float32
    )


def arrange(lines, owners, blocks, places, width):
    _, groups, times, depth = lines[0].shape
    step = groups * times
    height = step * len(lines)
    count, slots = places.shape

    def kernel(owners_ref, blocks_ref, places_ref, *refs):
        high_ref, low_ref = refs[-2:]
        row = pl.program_id(0)
        for i, line_ref in enumerate(refs[:-2]):
            span = pl.ds(pl.multiple_of(owners_ref[i] * step, step), step)
            for slot in range(slots):
                at = places_ref[row * slots + slot]
                start = pl.multiple_of(jnp.maximum(at, 0) * width, width)
                part = line_ref[0, :, :, pl.ds(start, width)].reshape(step, width)
                high, low = split(jnp.where(at < 0, 0.0, part))
                high_ref[span, slot * width : (slot + 1) * width] = high
                low_ref[span, slot * width : (slot + 1) * width] = low

    shape = jax.ShapeDtypeStruct((count * height, slots * width), jnp.bfloat16)
    return pl.pallas_call(
        kernel,
        grid_spec=pltpu.PrefetchScalarGridSpec(
            num_scalar_prefetch=3,
            grid=(count,),
            in_specs=[
                pl.BlockSpec(
                    (1, groups, times, depth), lambda i, owners, blocks, places: (blocks[i], 0, 0, 0)
                )
                for _ in lines
            ],
            out_specs=[
                pl.BlockSpec((height, slots * width), lambda i, owners, blocks, places: (i, 0))
            ]
            * 2,
        ),
        out_shape=[shape, shape],
        cost_estimate=pl.CostEstimate(flops=0, bytes_accessed=0, transcendentals=0),
    )(owners, blocks, places.reshape(-1), *lines)


def product(rows, pieces, modes, heights):
    depth = rows[0].shape[1]
    height = sum(heights)
    block = math.gcd(BLOCK, modes, *(start for _, start in pieces))
    count = len(pieces)

    def kernel(high_ref, low_ref, *refs):
        parts = [piece[...] for piece in refs[:count]]
        high, low = split(parts[0] if count == 1 else jnp.concatenate(parts, axis=1))
        at = 0
        for out_ref in refs[count:]:
            span = pl.ds(at, out_ref.shape[0])
            row_high = high_ref[span, :]
            out_ref[...] = dot(row_high, high) + (dot(row_high, low) + dot(low_ref[span, :], high))
            at += out_ref.shape[0]

    return pl.pallas_call(
        kernel,
        grid=(modes // block,),
        in_specs=[pl.BlockSpec((height, depth), lambda i: (0, 0))] * 2
        + [
            pl.BlockSpec((block, x.shape[1]), lambda i, first=start // block: (first + i, 0))
            for x, start in pieces
        ],
        out_specs=[pl.BlockSpec((h, block), lambda i: (0, i)) for h in heights],
        out_shape=[jax.ShapeDtypeStruct((h, modes), jnp.float32) for h in heights],
        compiler_params=pltpu.CompilerParams(vmem_limit_bytes=48 * 2**20),
        cost_estimate=pl.CostEstimate(flops=0, bytes_accessed=0, transcendentals=0),
    )(*rows, *(x for x, _ in pieces))


def put(out, parts, start, modes):
    height, span = parts[0].shape
    block = math.gcd(math.gcd(4 * BLOCK, span), start or span)
    first = start // block
    count = len(parts)

    def kernel(*refs):
        value = refs[0][...]
        for ref in refs[1:count]:
            value = value + ref[...]
        refs[-1][...] = value

    operands = list(parts)
    in_specs = [pl.BlockSpec((height, block), lambda i: (0, i)) for _ in parts]
    if out is not None:
        operands.append(out)
        in_specs.append(pl.BlockSpec(memory_space=pltpu.HBM))
    return pl.pallas_call(
        kernel,
        grid=(span // block,),
        in_specs=in_specs,
        out_specs=pl.BlockSpec((height, block), lambda i: (0, first + i)),
        out_shape=jax.ShapeDtypeStruct((height, modes), jnp.float32),
        input_output_aliases={} if out is None else {count: 0},
        compiler_params=pltpu.CompilerParams(vmem_limit_bytes=48 * 2**20),
        cost_estimate=pl.CostEstimate(flops=0, bytes_accessed=0, transcendentals=0),
    )(*operands)


def shards(snapshots, operator):
    chips = lax.axis_size("col") // CORES
    half = chips // 2
    modes, width = operator.shape
    col = lax.axis_index("col")
    chip, core = lax.div(col, CORES), lax.rem(col, CORES)
    side = (chip >= half).astype(jnp.int32)
    place = jnp.where(side == 0, half - 1 - chip, chip - half)

    def at(side, place):
        return (half - 1 - place) + side * (2 * place + 1)

    def move(x, routes, cross=0):
        pairs = [
            (at(a, i) * CORES + c, at(b, j) * CORES + (c + cross) % CORES)
            for (a, i), (b, j) in routes
            for c in range(CORES)
        ]
        return lax.ppermute(x, "col", pairs)

    def inward(x, i):
        return move(x, [((s, i), (s, 0)) for s in range(2)])

    def outward(x, i, cross=0):
        return move(x, [((s, 0), (s, i)) for s in range(2)], cross)

    def across(x, i=0, cross=0):
        return move(x, [((s, 0), (1 - s, i)) for s in range(2)], cross)

    def far(x, i):
        return move(x, [((s, i), (1 - s, 0)) for s in range(2)])

    def turn(x, i):
        return move(x, [((s, j), (s, (j + i) % half)) for s in range(2) for j in range(half)])

    def swap(x):
        return move(x, [((s, j), (s, j)) for s in range(2) for j in range(half)], 1)

    edges = [0]
    for part in SIXTEENTHS:
        edges.append(edges[-1] + modes * part // sum(SIXTEENTHS))
    count = len(SIXTEENTHS)
    spokes = range(1, half)
    chunk = [operator[edges[k] : edges[k + 1]] for k in range(2)]

    def pair(x):
        if width % 128 == 0:
            return [(x, 0), (swap(x), 0)]
        other = swap(x)
        ends = jnp.where(core == 0, x, other), jnp.where(core == 0, other, x)
        return [(jnp.concatenate(ends, axis=1), 0)]

    def places_of(chips):
        if width % 128 == 0:
            return [q * CORES + e if q is not None else -1 for q in chips for e in (core, 1 - core)]
        return [-1 if q is None else q for q in chips]

    hub = across(chunk[0])
    first = [turn(chunk[1], i) for i in spokes]
    outer = [far(chunk[0], i) for i in spokes]
    rest = after(operator, hub)
    chunk += [rest[edges[k] : edges[k + 1]] for k in range(2, count)]
    if width % 128 == 0:
        other = swap(operator)
        own = [[(operator, edges[k]), (other, edges[k])] for k in range(count)]
    else:
        own = [pair(operator[edges[k] : edges[k + 1]]) for k in range(count)]

    turns = lax.axis_size("row")
    line_row = lax.axis_index("row")
    groups, times, _ = snapshots.shape
    line = lax.all_gather(snapshots, "col", axis=1, tiled=True)
    line = after(line, hub).reshape(groups, chips, CORES, times, -1)
    line = lax.dynamic_index_in_dim(line, core, axis=2, keepdims=False)
    line = jnp.swapaxes(line, 0, 1)
    lines = [line]
    for i in range(1, turns):
        lines.append(lax.ppermute(line, "row", [(r, (r + i) % turns) for r in range(turns)]))
    height = turns * groups * times

    def left_side(row_chips, places):
        rows = jnp.stack(row_chips).astype(jnp.int32)
        places = [places_of(chips) for chips in places]
        places = jnp.array([[jnp.asarray(x, jnp.int32) for x in row] for row in places])
        step = width if width % 128 == 0 else CORES * width
        owners = jnp.stack([lax.rem(line_row - i + turns, turns) for i in range(turns)])
        return arrange(lines, owners.astype(jnp.int32), rows, places, step)

    mine = [at(side, lax.rem(place + i, half)) for i in range(half)]
    others = [at(1 - side, i) for i in range(half)]
    columns = [at(side, lax.rem(place - i + half, half)) for i in range(half)]
    rows_a = left_side(
        mine,
        [
            [None if i and i == j else q for j, q in enumerate(mine + others)]
            for i in range(half)
        ],
    )
    rows_b = left_side([mine[0]] + others, [columns] * (1 + half))

    ready, totals, turned, lane = (hub,), [None], first, outer
    for k in range(1, count):
        if k == 2:
            turned = [turn(after(chunk[k], *outer, sums[0]), i) for i in spokes]
            inner = [inward(after(chunk[0], *turned), i) for i in spokes]
        elif k > 2:
            turned = [turn(after(chunk[k], *inner), i) for i in spokes]
        pieces = own[k] + [y for x in turned for y in pair(after(x, *ready))]
        sums = product(rows_b, pieces, edges[k + 1] - edges[k], [height] * (1 + half))
        sent = [None] * half
        for i in reversed(range(half)) if k == count - 1 else range(half):
            sent[i] = across(after(sums[1 + i], *lane), i)
            lane = [sent[i]]
        totals.append([sums[0], *sent])
        ready = (sums[0], sent[0])

    pieces = own[0] + [y for x in [*inner, hub, *outer] for y in pair(after(x, sums[0]))]
    sums = product(rows_a, pieces, edges[1], [height] * half)
    totals[0] = [sums[0]] + [outward(sums[i], i) for i in spokes]

    out = None
    for k in [*range(1, count - 1), 0, count - 1]:
        out = put(out, totals[k], edges[k], modes)
    return out.reshape(turns * groups, times, modes)


def solution(mesh):
    placed = (P("row", "col", None), P("row", "col"))
    return jax.shard_map(
        shards, mesh=mesh, in_specs=placed, out_specs=P(None, "col", "row"), check_vma=False
    )
```

```python
import math

import jax
import jax.numpy as jnp
from jax import lax
from jax.experimental import pallas as pl
from jax.experimental.pallas import tpu as pltpu
from jax.sharding import PartitionSpec as P

CORES = 2
BLOCK = 512
SIXTEENTHS = (4, 4, 4, 4)


def after(x, *others):
    return lax.optimization_barrier((x, *others))[0]


def split(x):
    high = x.astype(jnp.bfloat16)
    low = (x - high.astype(jnp.float32)).astype(jnp.bfloat16)
    return high, low


def dot(left, right):
    return lax.dot_general(
        left, right, (((1,), (1,)), ((), ())), preferred_element_type=jnp.float32
    )


def arrange(lines, owners, blocks, places, width):
    _, groups, times, depth = lines[0].shape
    step = groups * times
    height = step * len(lines)
    count, slots = places.shape

    def kernel(owners_ref, blocks_ref, places_ref, *refs):
        high_ref, low_ref = refs[-2:]
        row = pl.program_id(0)
        for i, line_ref in enumerate(refs[:-2]):
            span = pl.ds(pl.multiple_of(owners_ref[i] * step, step), step)
            for slot in range(slots):
                at = places_ref[row * slots + slot]
                start = pl.multiple_of(jnp.maximum(at, 0) * width, width)
                part = line_ref[0, :, :, pl.ds(start, width)].reshape(step, width)
                high, low = split(jnp.where(at < 0, 0.0, part))
                high_ref[span, slot * width : (slot + 1) * width] = high
                low_ref[span, slot * width : (slot + 1) * width] = low

    shape = jax.ShapeDtypeStruct((count * height, slots * width), jnp.bfloat16)
    return pl.pallas_call(
        kernel,
        grid_spec=pltpu.PrefetchScalarGridSpec(
            num_scalar_prefetch=3,
            grid=(count,),
            in_specs=[
                pl.BlockSpec(
                    (1, groups, times, depth), lambda i, owners, blocks, places: (blocks[i], 0, 0, 0)
                )
                for _ in lines
            ],
            out_specs=[
                pl.BlockSpec((height, slots * width), lambda i, owners, blocks, places: (i, 0))
            ]
            * 2,
        ),
        out_shape=[shape, shape],
        cost_estimate=pl.CostEstimate(flops=0, bytes_accessed=0, transcendentals=0),
    )(owners, blocks, places.reshape(-1), *lines)


def product(rows, pieces, modes, heights):
    depth = rows[0].shape[1]
    height = sum(heights)
    block = math.gcd(BLOCK, modes, *(start for _, start in pieces))
    count = len(pieces)

    def kernel(high_ref, low_ref, *refs):
        parts = [piece[...] for piece in refs[:count]]
        high, low = split(parts[0] if count == 1 else jnp.concatenate(parts, axis=1))
        at = 0
        for out_ref in refs[count:]:
            span = pl.ds(at, out_ref.shape[0])
            row_high = high_ref[span, :]
            out_ref[...] = dot(row_high, high) + (dot(row_high, low) + dot(low_ref[span, :], high))
            at += out_ref.shape[0]

    return pl.pallas_call(
        kernel,
        grid=(modes // block,),
        in_specs=[pl.BlockSpec((height, depth), lambda i: (0, 0))] * 2
        + [
            pl.BlockSpec((block, x.shape[1]), lambda i, first=start // block: (first + i, 0))
            for x, start in pieces
        ],
        out_specs=[pl.BlockSpec((h, block), lambda i: (0, i)) for h in heights],
        out_shape=[jax.ShapeDtypeStruct((h, modes), jnp.float32) for h in heights],
        compiler_params=pltpu.CompilerParams(vmem_limit_bytes=48 * 2**20),
        cost_estimate=pl.CostEstimate(flops=0, bytes_accessed=0, transcendentals=0),
    )(*rows, *(x for x, _ in pieces))


def put(out, parts, start, modes):
    height, span = parts[0].shape
    block = math.gcd(math.gcd(4 * BLOCK, span), start or span)
    first = start // block
    count = len(parts)

    def kernel(*refs):
        value = refs[0][...]
        for ref in refs[1:count]:
            value = value + ref[...]
        refs[-1][...] = value

    operands = list(parts)
    in_specs = [pl.BlockSpec((height, block), lambda i: (0, i)) for _ in parts]
    if out is not None:
        operands.append(out)
        in_specs.append(pl.BlockSpec(memory_space=pltpu.HBM))
    return pl.pallas_call(
        kernel,
        grid=(span // block,),
        in_specs=in_specs,
        out_specs=pl.BlockSpec((height, block), lambda i: (0, first + i)),
        out_shape=jax.ShapeDtypeStruct((height, modes), jnp.float32),
        input_output_aliases={} if out is None else {count: 0},
        compiler_params=pltpu.CompilerParams(vmem_limit_bytes=48 * 2**20),
        cost_estimate=pl.CostEstimate(flops=0, bytes_accessed=0, transcendentals=0),
    )(*operands)


def shards(snapshots, operator):
    chips = lax.axis_size("col") // CORES
    half = chips // 2
    modes, width = operator.shape
    col = lax.axis_index("col")
    chip, core = lax.div(col, CORES), lax.rem(col, CORES)
    side = (chip >= half).astype(jnp.int32)
    place = jnp.where(side == 0, half - 1 - chip, chip - half)

    def at(side, place):
        return (half - 1 - place) + side * (2 * place + 1)

    def move(x, routes, cross=0):
        pairs = [
            (at(a, i) * CORES + c, at(b, j) * CORES + (c + cross) % CORES)
            for (a, i), (b, j) in routes
            for c in range(CORES)
        ]
        return lax.ppermute(x, "col", pairs)

    def inward(x, i):
        return move(x, [((s, i), (s, 0)) for s in range(2)])

    def outward(x, i, cross=0):
        return move(x, [((s, 0), (s, i)) for s in range(2)], cross)

    def across(x, i=0, cross=0):
        return move(x, [((s, 0), (1 - s, i)) for s in range(2)], cross)

    def far(x, i):
        return move(x, [((s, i), (1 - s, 0)) for s in range(2)])

    def turn(x, i):
        return move(x, [((s, j), (s, (j + i) % half)) for s in range(2) for j in range(half)])

    def swap(x):
        return move(x, [((s, j), (s, j)) for s in range(2) for j in range(half)], 1)

    edges = [0]
    for part in SIXTEENTHS:
        edges.append(edges[-1] + modes * part // sum(SIXTEENTHS))
    count = len(SIXTEENTHS)
    spokes = range(1, half)
    chunk = [operator[edges[k] : edges[k + 1]] for k in range(2)]

    def pair(x):
        if width % 128 == 0:
            return [(x, 0), (swap(x), 0)]
        other = swap(x)
        ends = jnp.where(core == 0, x, other), jnp.where(core == 0, other, x)
        return [(jnp.concatenate(ends, axis=1), 0)]

    def places_of(chips):
        if width % 128 == 0:
            return [q * CORES + e if q is not None else -1 for q in chips for e in (core, 1 - core)]
        return [-1 if q is None else q for q in chips]

    hub = across(chunk[0])
    first = [turn(chunk[1], i) for i in spokes]
    near = [snapshots] + [turn(snapshots, i) for i in reversed(spokes)]
    line = jnp.stack(near + [across(snapshots)] + [far(snapshots, i) for i in spokes])
    outer = [far(after(chunk[0], line), i) for i in spokes]
    rest = after(operator, hub)
    chunk += [rest[edges[k] : edges[k + 1]] for k in range(2, count)]
    if width % 128 == 0:
        other = swap(operator)
        own = [[(operator, edges[k]), (other, edges[k])] for k in range(count)]
    else:
        own = [pair(operator[edges[k] : edges[k + 1]]) for k in range(count)]

    turns = lax.axis_size("row")
    line_row = lax.axis_index("row")
    groups, times, _ = snapshots.shape
    lines = [line]
    for i in range(1, turns):
        lines.append(lax.ppermute(line, "row", [(r, (r + i) % turns) for r in range(turns)]))
    height = turns * groups * times

    def left_side(row_chips, places):
        rows = jnp.array(row_chips, jnp.int32)
        places = [places_of(chips) for chips in places]
        places = jnp.array([[jnp.asarray(x, jnp.int32) for x in row] for row in places])
        step = width if width % 128 == 0 else CORES * width
        owners = jnp.stack([lax.rem(line_row - i + turns, turns) for i in range(turns)])
        return arrange(lines, owners.astype(jnp.int32), rows, places, step)

    mine = [at(side, lax.rem(place + i, half)) for i in range(half)]
    others = [at(1 - side, i) for i in range(half)]
    columns = [at(side, lax.rem(place - i + half, half)) for i in range(half)]
    rows_a = left_side(
        range(half),
        [
            [None if i and i == j else q for j, q in enumerate(mine + others)]
            for i in range(half)
        ],
    )
    rows_b = left_side([0, *range(half, 2 * half)], [columns] * (1 + half))

    ready, totals, turned, lane = (hub,), [None], first, outer
    for k in range(1, count):
        if k == 2:
            turned = [turn(after(chunk[k], *outer, sums[0]), i) for i in spokes]
            inner = [inward(after(chunk[0], *turned), i) for i in spokes]
        elif k > 2:
            turned = [turn(after(chunk[k], *inner), i) for i in spokes]
        pieces = own[k] + [y for x in turned for y in pair(after(x, *ready))]
        sums = product(rows_b, pieces, edges[k + 1] - edges[k], [height] * (1 + half))
        sent = [None] * half
        for i in reversed(range(half)) if k == count - 1 else range(half):
            sent[i] = across(after(sums[1 + i], *lane), i)
            lane = [sent[i]]
        totals.append([sums[0], *sent])
        ready = (sums[0], sent[0])

    pieces = own[0] + [y for x in [*inner, hub, *outer] for y in pair(after(x, sums[0]))]
    sums = product(rows_a, pieces, edges[1], [height] * half)
    totals[0] = [sums[0]] + [outward(sums[i], i) for i in spokes]

    out = None
    for k in [*range(1, count - 1), 0, count - 1]:
        out = put(out, totals[k], edges[k], modes)
    return out.reshape(turns * groups, times, modes)


def solution(mesh):
    placed = (P("row", "col", None), P("row", "col"))
    return jax.shard_map(
        shards, mesh=mesh, in_specs=placed, out_specs=P(None, "col", "row"), check_vma=False
    )
```

```python
import math

import jax
import jax.numpy as jnp
from jax import lax
from jax.experimental import pallas as pl
from jax.experimental.pallas import tpu as pltpu
from jax.sharding import PartitionSpec as P

CORES = 2
BLOCK = 512
SIXTEENTHS = (4, 4, 4, 4)


def after(x, *others):
    return lax.optimization_barrier((x, *others))[0]


def split(x):
    high = x.astype(jnp.bfloat16)
    low = (x - high.astype(jnp.float32)).astype(jnp.bfloat16)
    return high, low


def dot(left, right):
    return lax.dot_general(
        left, right, (((1,), (1,)), ((), ())), preferred_element_type=jnp.float32
    )


def arrange(lines, owners, blocks, places, width):
    _, groups, times, depth = lines[0].shape
    step = groups * times
    height = step * len(lines)
    count, slots = places.shape

    def kernel(owners_ref, blocks_ref, places_ref, *refs):
        high_ref, low_ref = refs[-2:]
        row = pl.program_id(0)
        for i, line_ref in enumerate(refs[:-2]):
            span = pl.ds(pl.multiple_of(owners_ref[i] * step, step), step)
            for slot in range(slots):
                at = places_ref[row * slots + slot]
                start = pl.multiple_of(jnp.maximum(at, 0) * width, width)
                part = line_ref[0, :, :, pl.ds(start, width)].reshape(step, width)
                high, low = split(jnp.where(at < 0, 0.0, part))
                high_ref[span, slot * width : (slot + 1) * width] = high
                low_ref[span, slot * width : (slot + 1) * width] = low

    shape = jax.ShapeDtypeStruct((count * height, slots * width), jnp.bfloat16)
    return pl.pallas_call(
        kernel,
        grid_spec=pltpu.PrefetchScalarGridSpec(
            num_scalar_prefetch=3,
            grid=(count,),
            in_specs=[
                pl.BlockSpec(
                    (1, groups, times, depth), lambda i, owners, blocks, places: (blocks[i], 0, 0, 0)
                )
                for _ in lines
            ],
            out_specs=[
                pl.BlockSpec((height, slots * width), lambda i, owners, blocks, places: (i, 0))
            ]
            * 2,
        ),
        out_shape=[shape, shape],
        cost_estimate=pl.CostEstimate(flops=0, bytes_accessed=0, transcendentals=0),
    )(owners, blocks, places.reshape(-1), *lines)


def product(rows, pieces, modes, heights):
    depth = rows[0].shape[1]
    height = sum(heights)
    block = math.gcd(BLOCK, modes, *(start for _, start in pieces))
    count = len(pieces)

    def kernel(high_ref, low_ref, *refs):
        parts = [piece[...] for piece in refs[:count]]
        high, low = split(parts[0] if count == 1 else jnp.concatenate(parts, axis=1))
        at = 0
        for out_ref in refs[count:]:
            span = pl.ds(at, out_ref.shape[0])
            row_high = high_ref[span, :]
            out_ref[...] = dot(row_high, high) + (dot(row_high, low) + dot(low_ref[span, :], high))
            at += out_ref.shape[0]

    return pl.pallas_call(
        kernel,
        grid=(modes // block,),
        in_specs=[pl.BlockSpec((height, depth), lambda i: (0, 0))] * 2
        + [
            pl.BlockSpec((block, x.shape[1]), lambda i, first=start // block: (first + i, 0))
            for x, start in pieces
        ],
        out_specs=[pl.BlockSpec((h, block), lambda i: (0, i)) for h in heights],
        out_shape=[jax.ShapeDtypeStruct((h, modes), jnp.float32) for h in heights],
        compiler_params=pltpu.CompilerParams(vmem_limit_bytes=48 * 2**20),
        cost_estimate=pl.CostEstimate(flops=0, bytes_accessed=0, transcendentals=0),
    )(*rows, *(x for x, _ in pieces))


def put(out, parts, start, modes):
    height, span = parts[0].shape
    block = math.gcd(math.gcd(4 * BLOCK, span), start or span)
    first = start // block
    count = len(parts)

    def kernel(*refs):
        value = refs[0][...]
        for ref in refs[1:count]:
            value = value + ref[...]
        refs[-1][...] = value

    operands = list(parts)
    in_specs = [pl.BlockSpec((height, block), lambda i: (0, i)) for _ in parts]
    if out is not None:
        operands.append(out)
        in_specs.append(pl.BlockSpec(memory_space=pltpu.HBM))
    return pl.pallas_call(
        kernel,
        grid=(span // block,),
        in_specs=in_specs,
        out_specs=pl.BlockSpec((height, block), lambda i: (0, first + i)),
        out_shape=jax.ShapeDtypeStruct((height, modes), jnp.float32),
        input_output_aliases={} if out is None else {count: 0},
        compiler_params=pltpu.CompilerParams(vmem_limit_bytes=48 * 2**20),
        cost_estimate=pl.CostEstimate(flops=0, bytes_accessed=0, transcendentals=0),
    )(*operands)


def shards(snapshots, operator):
    chips = lax.axis_size("col") // CORES
    half = chips // 2
    modes, width = operator.shape
    col = lax.axis_index("col")
    chip, core = lax.div(col, CORES), lax.rem(col, CORES)
    side = (chip >= half).astype(jnp.int32)
    place = jnp.where(side == 0, half - 1 - chip, chip - half)

    def at(side, place):
        return (half - 1 - place) + side * (2 * place + 1)

    def move(x, routes, cross=0):
        pairs = [
            (at(a, i) * CORES + c, at(b, j) * CORES + (c + cross) % CORES)
            for (a, i), (b, j) in routes
            for c in range(CORES)
        ]
        return lax.ppermute(x, "col", pairs)

    def inward(x, i):
        return move(x, [((s, i), (s, 0)) for s in range(2)])

    def outward(x, i, cross=0):
        return move(x, [((s, 0), (s, i)) for s in range(2)], cross)

    def across(x, i=0, cross=0):
        return move(x, [((s, 0), (1 - s, i)) for s in range(2)], cross)

    def far(x, i):
        return move(x, [((s, i), (1 - s, 0)) for s in range(2)])

    def turn(x, i):
        return move(x, [((s, j), (s, (j + i) % half)) for s in range(2) for j in range(half)])

    def swap(x):
        return move(x, [((s, j), (s, j)) for s in range(2) for j in range(half)], 1)

    edges = [0]
    for part in SIXTEENTHS:
        edges.append(edges[-1] + modes * part // sum(SIXTEENTHS))
    count = len(SIXTEENTHS)
    spokes = range(1, half)
    chunk = [operator[edges[k] : edges[k + 1]] for k in range(2)]

    def pair(x):
        if width % 128 == 0:
            return [(x, 0), (swap(x), 0)]
        other = swap(x)
        ends = jnp.where(core == 0, x, other), jnp.where(core == 0, other, x)
        return [(jnp.concatenate(ends, axis=1), 0)]

    def places_of(chips):
        if width % 128 == 0:
            return [q * CORES + e if q is not None else -1 for q in chips for e in (core, 1 - core)]
        return [-1 if q is None else q for q in chips]

    hub = across(chunk[0])
    first = [turn(chunk[1], i) for i in spokes]
    near = [snapshots] + [turn(snapshots, i) for i in reversed(spokes)]
    line = jnp.stack(near + [across(snapshots)] + [far(snapshots, i) for i in spokes])
    outer = [far(after(chunk[0], line), i) for i in spokes]
    rest = after(operator, hub)
    chunk += [rest[edges[k] : edges[k + 1]] for k in range(2, count)]
    turns = lax.axis_size("row")
    line_row = lax.axis_index("row")
    groups, times, _ = snapshots.shape
    lines = [line]
    for i in range(1, turns):
        lines.append(lax.ppermute(line, "row", [(r, (r + i) % turns) for r in range(turns)]))
    height = turns * groups * times

    def left_side(row_chips, places):
        rows = jnp.array(row_chips, jnp.int32)
        places = [places_of(chips) for chips in places]
        places = jnp.array([[jnp.asarray(x, jnp.int32) for x in row] for row in places])
        step = width if width % 128 == 0 else CORES * width
        owners = jnp.stack([lax.rem(line_row - i + turns, turns) for i in range(turns)])
        return arrange(lines, owners.astype(jnp.int32), rows, places, step)

    mine = [at(side, lax.rem(place + i, half)) for i in range(half)]
    others = [at(1 - side, i) for i in range(half)]
    columns = [at(side, lax.rem(place - i + half, half)) for i in range(half)]
    rows_a = left_side(
        range(half),
        [
            [None if i and i == j else q for j, q in enumerate(mine + others)]
            for i in range(half)
        ],
    )
    rows_b = left_side([0, *range(half, 2 * half)], [columns] * (1 + half))

    ready, totals, turned, lane = (hub,), [None], first, ()
    for k in range(1, count):
        if k == 2:
            turned = [turn(after(chunk[k], *outer, sums[0]), i) for i in spokes]
            inner = [inward(after(chunk[0], *turned), i) for i in spokes]
        elif k > 2:
            turned = [turn(after(chunk[k], *inner), i) for i in spokes]
        pieces = [y for x in [chunk[k], *turned] for y in pair(after(x, *ready))]
        sums = product(rows_b, pieces, edges[k + 1] - edges[k], [height] * (1 + half))
        sent = [None] * half
        for i in reversed(range(half)) if k == count - 1 else range(half):
            sent[i] = across(after(sums[1 + i], *lane), i)
            lane = [sent[i]]
        totals.append([sums[0], *sent])
        ready = (sums[0], sent[0])

    pieces = [y for x in [chunk[0], *inner, hub, *outer] for y in pair(after(x, sums[0]))]
    sums = product(rows_a, pieces, edges[1], [height] * half)
    totals[0] = [sums[0]] + [outward(sums[i], i) for i in spokes]

    out = None
    for k in [*range(1, count - 1), 0, count - 1]:
        out = put(out, totals[k], edges[k], modes)
    return out.reshape(turns * groups, times, modes)


def solution(mesh):
    placed = (P("row", "col", None), P("row", "col"))
    return jax.shard_map(
        shards, mesh=mesh, in_specs=placed, out_specs=P(None, "col", "row"), check_vma=False
    )
```

```python
import math

import jax
import jax.numpy as jnp
from jax import lax
from jax.experimental import pallas as pl
from jax.experimental.pallas import tpu as pltpu
from jax.sharding import PartitionSpec as P

CORES = 2
BLOCK = 512
SIXTEENTHS = (4, 4, 4, 4)


def after(x, *others):
    return lax.optimization_barrier((x, *others))[0]


def split(x):
    high = x.astype(jnp.bfloat16)
    low = (x - high.astype(jnp.float32)).astype(jnp.bfloat16)
    return high, low


def dot(left, right):
    return lax.dot_general(
        left, right, (((1,), (1,)), ((), ())), preferred_element_type=jnp.float32
    )


def arrange(lines, owners, blocks, places, width):
    _, groups, times, depth = lines[0].shape
    step = groups * times
    height = step * len(lines)
    count, slots = places.shape

    def kernel(owners_ref, blocks_ref, places_ref, *refs):
        high_ref, low_ref = refs[-2:]
        row = pl.program_id(0)
        for i, line_ref in enumerate(refs[:-2]):
            span = pl.ds(pl.multiple_of(owners_ref[i] * step, step), step)
            for slot in range(slots):
                at = places_ref[row * slots + slot]
                start = pl.multiple_of(jnp.maximum(at, 0) * width, width)
                part = line_ref[0, :, :, pl.ds(start, width)].reshape(step, width)
                high, low = split(jnp.where(at < 0, 0.0, part))
                high_ref[span, slot * width : (slot + 1) * width] = high
                low_ref[span, slot * width : (slot + 1) * width] = low

    shape = jax.ShapeDtypeStruct((count * height, slots * width), jnp.bfloat16)
    return pl.pallas_call(
        kernel,
        grid_spec=pltpu.PrefetchScalarGridSpec(
            num_scalar_prefetch=3,
            grid=(count,),
            in_specs=[
                pl.BlockSpec(
                    (1, groups, times, depth), lambda i, owners, blocks, places: (blocks[i], 0, 0, 0)
                )
                for _ in lines
            ],
            out_specs=[
                pl.BlockSpec((height, slots * width), lambda i, owners, blocks, places: (i, 0))
            ]
            * 2,
        ),
        out_shape=[shape, shape],
        cost_estimate=pl.CostEstimate(flops=0, bytes_accessed=0, transcendentals=0),
    )(owners, blocks, places.reshape(-1), *lines)


def product(rows, pieces, modes, heights):
    depth = rows[0].shape[1]
    height = sum(heights)
    block = math.gcd(BLOCK, modes // 2, *(start for _, start in pieces))
    steps = modes // block
    widths = [len(arrays) for arrays, _ in pieces]
    operands, in_specs = [], []
    for arrays, start in pieces:
        first, size = start // block, steps // len(arrays)
        for j, x in enumerate(arrays):
            operands.append(x)
            in_specs.append(
                pl.BlockSpec(
                    (block, x.shape[1]),
                    lambda i, first=first, size=size, j=j: (
                        first + jnp.clip(i - j * size, 0, size - 1),
                        0,
                    ),
                )
            )
    count = len(operands)

    def kernel(high_ref, low_ref, *refs):
        parts, first = [], 0
        for size in widths:
            part = refs[first][...]
            if size == 2:
                early = pl.program_id(0) < steps // 2
                part = jnp.where(early, part, refs[first + 1][...])
            parts.append(part)
            first += size
        high, low = split(parts[0] if len(parts) == 1 else jnp.concatenate(parts, axis=1))
        at = 0
        for out_ref in refs[count:]:
            span = pl.ds(at, out_ref.shape[0])
            row_high = high_ref[span, :]
            out_ref[...] = dot(row_high, high) + (dot(row_high, low) + dot(low_ref[span, :], high))
            at += out_ref.shape[0]

    return pl.pallas_call(
        kernel,
        grid=(modes // block,),
        in_specs=[pl.BlockSpec((height, depth), lambda i: (0, 0))] * 2 + in_specs,
        out_specs=[pl.BlockSpec((h, block), lambda i: (0, i)) for h in heights],
        out_shape=[jax.ShapeDtypeStruct((h, modes), jnp.float32) for h in heights],
        compiler_params=pltpu.CompilerParams(vmem_limit_bytes=48 * 2**20),
        cost_estimate=pl.CostEstimate(flops=0, bytes_accessed=0, transcendentals=0),
    )(*rows, *operands)


def put(out, parts, start, modes):
    height, span = parts[0].shape
    block = math.gcd(math.gcd(4 * BLOCK, span), start or span)
    first = start // block
    count = len(parts)

    def kernel(*refs):
        value = refs[0][...]
        for ref in refs[1:count]:
            value = value + ref[...]
        refs[-1][...] = value

    operands = list(parts)
    in_specs = [pl.BlockSpec((height, block), lambda i: (0, i)) for _ in parts]
    if out is not None:
        operands.append(out)
        in_specs.append(pl.BlockSpec(memory_space=pltpu.HBM))
    return pl.pallas_call(
        kernel,
        grid=(span // block,),
        in_specs=in_specs,
        out_specs=pl.BlockSpec((height, block), lambda i: (0, first + i)),
        out_shape=jax.ShapeDtypeStruct((height, modes), jnp.float32),
        input_output_aliases={} if out is None else {count: 0},
        compiler_params=pltpu.CompilerParams(vmem_limit_bytes=48 * 2**20),
        cost_estimate=pl.CostEstimate(flops=0, bytes_accessed=0, transcendentals=0),
    )(*operands)


def shards(snapshots, operator):
    chips = lax.axis_size("col") // CORES
    half = chips // 2
    modes, width = operator.shape
    col = lax.axis_index("col")
    chip, core = lax.div(col, CORES), lax.rem(col, CORES)
    side = (chip >= half).astype(jnp.int32)
    place = jnp.where(side == 0, half - 1 - chip, chip - half)

    def at(side, place):
        return (half - 1 - place) + side * (2 * place + 1)

    def move(x, routes, cross=0):
        pairs = [
            (at(a, i) * CORES + c, at(b, j) * CORES + (c + cross) % CORES)
            for (a, i), (b, j) in routes
            for c in range(CORES)
        ]
        return lax.ppermute(x, "col", pairs)

    def inward(x, i):
        return move(x, [((s, i), (s, 0)) for s in range(2)])

    def outward(x, i, cross=0):
        return move(x, [((s, 0), (s, i)) for s in range(2)], cross)

    def across(x, i=0, cross=0):
        return move(x, [((s, 0), (1 - s, i)) for s in range(2)], cross)

    def far(x, i):
        return move(x, [((s, i), (1 - s, 0)) for s in range(2)])

    def turn(x, i):
        return move(x, [((s, j), (s, (j + i) % half)) for s in range(2) for j in range(half)])

    def swap(x):
        return move(x, [((s, j), (s, j)) for s in range(2) for j in range(half)], 1)

    edges = [0]
    for part in SIXTEENTHS:
        edges.append(edges[-1] + modes * part // sum(SIXTEENTHS))
    count = len(SIXTEENTHS)
    spokes = range(1, half)
    chunk = [operator[edges[k] : edges[k + 1]] for k in range(2)]

    def pair(x, cut=False):
        if width % 128 == 0:
            middle = x.shape[0] // 2
            ends = (x[:middle], x[middle:]) if cut else (x,)
            return [((x,), 0), (tuple(swap(end) for end in ends), 0)]
        other = swap(x)
        ends = jnp.where(core == 0, x, other), jnp.where(core == 0, other, x)
        return [((jnp.concatenate(ends, axis=1),), 0)]

    def places_of(chips):
        if width % 128 == 0:
            return [q * CORES + e if q is not None else -1 for q in chips for e in (core, 1 - core)]
        return [-1 if q is None else q for q in chips]

    hub = across(chunk[0])
    first = [turn(chunk[1], i) for i in spokes]
    near = [snapshots] + [turn(snapshots, i) for i in reversed(spokes)]
    line = jnp.stack(near + [across(snapshots)] + [far(snapshots, i) for i in spokes])
    outer = [far(after(chunk[0], line), i) for i in spokes]
    rest = after(operator, hub)
    chunk += [rest[edges[k] : edges[k + 1]] for k in range(2, count)]
    turns = lax.axis_size("row")
    line_row = lax.axis_index("row")
    groups, times, _ = snapshots.shape
    lines = [line]
    for i in range(1, turns):
        lines.append(lax.ppermute(line, "row", [(r, (r + i) % turns) for r in range(turns)]))
    height = turns * groups * times

    def left_side(row_chips, places):
        rows = jnp.array(row_chips, jnp.int32)
        places = [places_of(chips) for chips in places]
        places = jnp.array([[jnp.asarray(x, jnp.int32) for x in row] for row in places])
        step = width if width % 128 == 0 else CORES * width
        owners = jnp.stack([lax.rem(line_row - i + turns, turns) for i in range(turns)])
        return arrange(lines, owners.astype(jnp.int32), rows, places, step)

    mine = [at(side, lax.rem(place + i, half)) for i in range(half)]
    others = [at(1 - side, i) for i in range(half)]
    columns = [at(side, lax.rem(place - i + half, half)) for i in range(half)]
    rows_a = left_side(
        range(half),
        [
            [None if i and i == j else q for j, q in enumerate(mine + others)]
            for i in range(half)
        ],
    )
    rows_b = left_side([0, *range(half, 2 * half)], [columns] * (1 + half))

    ready, totals, turned, lane = (hub,), [None], first, ()
    for k in range(1, count):
        if k == 2:
            turned = [turn(after(chunk[k], *outer, sums[0]), i) for i in spokes]
            inner = [inward(after(chunk[0], *turned), i) for i in spokes]
        elif k > 2:
            turned = [turn(after(chunk[k], *inner), i) for i in spokes]
        pieces = pair(after(chunk[k], *ready) if k == 1 else chunk[k])
        pieces += [y for x in turned for y in pair(after(x, *ready), k > 1)]
        sums = product(rows_b, pieces, edges[k + 1] - edges[k], [height] * (1 + half))
        sent = [None] * half
        for i in reversed(range(half)) if k == count - 1 else range(half):
            sent[i] = across(after(sums[1 + i], *lane), i)
        lane = sent[-1:] if k < count - 1 else ()
        totals.append([sums[0], *sent])
        ready = (sums[0], sent[0])

    pieces = [y for x in [chunk[0], *inner, hub, *outer] for y in pair(after(x, sums[0]))]
    sums = product(rows_a, pieces, edges[1], [height] * half)
    totals[0] = [sums[0]] + [outward(sums[i], i) for i in spokes]

    out = None
    for k in [*range(1, count - 1), 0, count - 1]:
        out = put(out, totals[k], edges[k], modes)
    return out.reshape(turns * groups, times, modes)


def solution(mesh):
    placed = (P("row", "col", None), P("row", "col"))
    return jax.shard_map(
        shards, mesh=mesh, in_specs=placed, out_specs=P(None, "col", "row"), check_vma=False
    )
```

```python
import math

import jax
import jax.numpy as jnp
from jax import lax
from jax.experimental import pallas as pl
from jax.experimental.pallas import tpu as pltpu
from jax.sharding import PartitionSpec as P

CORES = 2
BLOCK = 512
SIXTEENTHS = (4, 4, 4, 4)


def after(x, *others):
    return lax.optimization_barrier((x, *others))[0]


def split(x):
    high = x.astype(jnp.bfloat16)
    low = (x - high.astype(jnp.float32)).astype(jnp.bfloat16)
    return high, low


def dot(left, right):
    return lax.dot_general(
        left, right, (((1,), (1,)), ((), ())), preferred_element_type=jnp.float32
    )


def arrange(lines, owners, blocks, places, width):
    _, groups, times, depth = lines[0].shape
    step = groups * times
    height = step * len(lines)
    count, slots = places.shape

    def kernel(owners_ref, blocks_ref, places_ref, *refs):
        high_ref, low_ref = refs[-2:]
        row = pl.program_id(0)
        for i, line_ref in enumerate(refs[:-2]):
            span = pl.ds(pl.multiple_of(owners_ref[i] * step, step), step)
            for slot in range(slots):
                at = places_ref[row * slots + slot]
                start = pl.multiple_of(jnp.maximum(at, 0) * width, width)
                part = line_ref[0, :, :, pl.ds(start, width)].reshape(step, width)
                high, low = split(jnp.where(at < 0, 0.0, part))
                high_ref[span, slot * width : (slot + 1) * width] = high
                low_ref[span, slot * width : (slot + 1) * width] = low

    shape = jax.ShapeDtypeStruct((count * height, slots * width), jnp.bfloat16)
    return pl.pallas_call(
        kernel,
        grid_spec=pltpu.PrefetchScalarGridSpec(
            num_scalar_prefetch=3,
            grid=(count,),
            in_specs=[
                pl.BlockSpec(
                    (1, groups, times, depth), lambda i, owners, blocks, places: (blocks[i], 0, 0, 0)
                )
                for _ in lines
            ],
            out_specs=[
                pl.BlockSpec((height, slots * width), lambda i, owners, blocks, places: (i, 0))
            ]
            * 2,
        ),
        out_shape=[shape, shape],
        cost_estimate=pl.CostEstimate(flops=0, bytes_accessed=0, transcendentals=0),
    )(owners, blocks, places.reshape(-1), *lines)


def product(rows, pieces, modes, heights):
    depth = rows[0].shape[1]
    height = sum(heights)
    block = math.gcd(BLOCK, modes // 2, *(start for _, start in pieces))
    steps = modes // block
    widths = [len(arrays) for arrays, _ in pieces]
    operands, in_specs = [], []
    for arrays, start in pieces:
        first, size = start // block, steps // len(arrays)
        for j, x in enumerate(arrays):
            operands.append(x)
            in_specs.append(
                pl.BlockSpec(
                    (block, x.shape[1]),
                    lambda i, first=first, size=size, j=j: (
                        first + jnp.clip(i - j * size, 0, size - 1),
                        0,
                    ),
                )
            )
    count = len(operands)

    def kernel(high_ref, low_ref, *refs):
        parts, first = [], 0
        for size in widths:
            part = refs[first][...]
            if size == 2:
                early = pl.program_id(0) < steps // 2
                part = jnp.where(early, part, refs[first + 1][...])
            parts.append(part)
            first += size
        high, low = split(parts[0] if len(parts) == 1 else jnp.concatenate(parts, axis=1))
        at = 0
        for out_ref in refs[count:]:
            span = pl.ds(at, out_ref.shape[0])
            row_high = high_ref[span, :]
            out_ref[...] = dot(row_high, high) + (dot(row_high, low) + dot(low_ref[span, :], high))
            at += out_ref.shape[0]

    return pl.pallas_call(
        kernel,
        grid=(modes // block,),
        in_specs=[pl.BlockSpec((height, depth), lambda i: (0, 0))] * 2 + in_specs,
        out_specs=[pl.BlockSpec((h, block), lambda i: (0, i)) for h in heights],
        out_shape=[jax.ShapeDtypeStruct((h, modes), jnp.float32) for h in heights],
        compiler_params=pltpu.CompilerParams(vmem_limit_bytes=48 * 2**20),
        cost_estimate=pl.CostEstimate(flops=0, bytes_accessed=0, transcendentals=0),
    )(*rows, *operands)


def put(out, parts, start, modes):
    height, span = parts[0].shape
    block = math.gcd(math.gcd(8 * BLOCK, span), start or span)
    first = start // block
    count = len(parts)

    def kernel(*refs):
        value = refs[0][...]
        for ref in refs[1:count]:
            value = value + ref[...]
        refs[-1][...] = value

    operands = list(parts)
    in_specs = [pl.BlockSpec((height, block), lambda i: (0, i)) for _ in parts]
    if out is not None:
        operands.append(out)
        in_specs.append(pl.BlockSpec(memory_space=pltpu.HBM))
    return pl.pallas_call(
        kernel,
        grid=(span // block,),
        in_specs=in_specs,
        out_specs=pl.BlockSpec((height, block), lambda i: (0, first + i)),
        out_shape=jax.ShapeDtypeStruct((height, modes), jnp.float32),
        input_output_aliases={} if out is None else {count: 0},
        compiler_params=pltpu.CompilerParams(vmem_limit_bytes=48 * 2**20),
        cost_estimate=pl.CostEstimate(flops=0, bytes_accessed=0, transcendentals=0),
    )(*operands)


def shards(snapshots, operator):
    chips = lax.axis_size("col") // CORES
    half = chips // 2
    modes, width = operator.shape
    col = lax.axis_index("col")
    chip, core = lax.div(col, CORES), lax.rem(col, CORES)
    side = (chip >= half).astype(jnp.int32)
    place = jnp.where(side == 0, half - 1 - chip, chip - half)

    def at(side, place):
        return (half - 1 - place) + side * (2 * place + 1)

    def move(x, routes, cross=0):
        pairs = [
            (at(a, i) * CORES + c, at(b, j) * CORES + (c + cross) % CORES)
            for (a, i), (b, j) in routes
            for c in range(CORES)
        ]
        return lax.ppermute(x, "col", pairs)

    def inward(x, i):
        return move(x, [((s, i), (s, 0)) for s in range(2)])

    def outward(x, i, cross=0):
        return move(x, [((s, 0), (s, i)) for s in range(2)], cross)

    def across(x, i=0, cross=0):
        return move(x, [((s, 0), (1 - s, i)) for s in range(2)], cross)

    def far(x, i):
        return move(x, [((s, i), (1 - s, 0)) for s in range(2)])

    def turn(x, i):
        return move(x, [((s, j), (s, (j + i) % half)) for s in range(2) for j in range(half)])

    def swap(x):
        return move(x, [((s, j), (s, j)) for s in range(2) for j in range(half)], 1)

    edges = [0]
    for part in SIXTEENTHS:
        edges.append(edges[-1] + modes * part // sum(SIXTEENTHS))
    count = len(SIXTEENTHS)
    spokes = range(1, half)
    chunk = [operator[edges[k] : edges[k + 1]] for k in range(2)]

    def pair(x, cut=False):
        if width % 128 == 0:
            middle = x.shape[0] // 2
            ends = (x[:middle], x[middle:]) if cut else (x,)
            return [((x,), 0), (tuple(swap(end) for end in ends), 0)]
        other = swap(x)
        ends = jnp.where(core == 0, x, other), jnp.where(core == 0, other, x)
        return [((jnp.concatenate(ends, axis=1),), 0)]

    def places_of(chips):
        if width % 128 == 0:
            return [q * CORES + e if q is not None else -1 for q in chips for e in (core, 1 - core)]
        return [-1 if q is None else q for q in chips]

    hub = across(chunk[0])
    first = [turn(chunk[1], i) for i in spokes]
    near = [snapshots] + [turn(snapshots, i) for i in reversed(spokes)]
    line = jnp.stack(near + [across(snapshots)] + [far(snapshots, i) for i in spokes])
    outer = [far(after(chunk[0], line), i) for i in spokes]
    rest = after(operator, hub)
    chunk += [rest[edges[k] : edges[k + 1]] for k in range(2, count)]
    turns = lax.axis_size("row")
    line_row = lax.axis_index("row")
    groups, times, _ = snapshots.shape
    lines = [line]
    for i in range(1, turns):
        lines.append(lax.ppermute(line, "row", [(r, (r + i) % turns) for r in range(turns)]))
    height = turns * groups * times

    def left_side(row_chips, places):
        rows = jnp.array(row_chips, jnp.int32)
        places = [places_of(chips) for chips in places]
        places = jnp.array([[jnp.asarray(x, jnp.int32) for x in row] for row in places])
        step = width if width % 128 == 0 else CORES * width
        owners = jnp.stack([lax.rem(line_row - i + turns, turns) for i in range(turns)])
        return arrange(lines, owners.astype(jnp.int32), rows, places, step)

    mine = [at(side, lax.rem(place + i, half)) for i in range(half)]
    others = [at(1 - side, i) for i in range(half)]
    columns = [at(side, lax.rem(place - i + half, half)) for i in range(half)]
    rows_a = left_side(
        range(half),
        [
            [None if i and i == j else q for j, q in enumerate(mine + others)]
            for i in range(half)
        ],
    )
    rows_b = left_side([0, *range(half, 2 * half)], [columns] * (1 + half))

    ready, totals, turned, lane = (hub,), [None], first, ()
    for k in range(1, count):
        if k == 2:
            turned = [turn(after(chunk[k], *outer, sums[0]), i) for i in spokes]
            inner = [inward(after(chunk[0], *turned), i) for i in spokes]
        elif k > 2:
            turned = [turn(after(chunk[k], *inner), i) for i in spokes]
        pieces = pair(after(chunk[k], *ready) if k == 1 else chunk[k])
        pieces += [y for x in turned for y in pair(after(x, *ready), k > 1)]
        sums = product(rows_b, pieces, edges[k + 1] - edges[k], [height] * (1 + half))
        sent = [None] * half
        for i in reversed(range(half)) if k == count - 1 else range(half):
            sent[i] = across(after(sums[1 + i], *lane), i)
        lane = sent[-1:] if k < count - 1 else ()
        totals.append([sums[0], *sent])
        ready = (sums[0], sent[0])

    pieces = [y for x in [chunk[0], *inner, hub, *outer] for y in pair(after(x, sums[0]))]
    sums = product(rows_a, pieces, edges[1], [height] * half)
    totals[0] = [sums[0]] + [outward(sums[i], i) for i in spokes]

    out = None
    for k in [*range(1, count - 1), 0, count - 1]:
        out = put(out, totals[k], edges[k], modes)
    return out.reshape(turns * groups, times, modes)


def solution(mesh):
    placed = (P("row", "col", None), P("row", "col"))
    return jax.shard_map(
        shards, mesh=mesh, in_specs=placed, out_specs=P(None, "col", "row"), check_vma=False
    )
```

```python
import math

import jax
import jax.numpy as jnp
from jax import lax
from jax.experimental import pallas as pl
from jax.experimental.pallas import tpu as pltpu
from jax.sharding import PartitionSpec as P

CORES = 2
BLOCK = 1024
SIXTEENTHS = (4, 4, 4, 4)


def after(x, *others):
    return lax.optimization_barrier((x, *others))[0]


def split(x):
    high = x.astype(jnp.bfloat16)
    low = (x - high.astype(jnp.float32)).astype(jnp.bfloat16)
    return high, low


def dot(left, right):
    return lax.dot_general(
        left, right, (((1,), (1,)), ((), ())), preferred_element_type=jnp.float32
    )


def arrange(lines, owners, blocks, places, width):
    _, groups, times, depth = lines[0].shape
    step = groups * times
    height = step * len(lines)
    count, slots = places.shape

    def kernel(owners_ref, blocks_ref, places_ref, *refs):
        high_ref, low_ref = refs[-2:]
        row = pl.program_id(0)
        for i, line_ref in enumerate(refs[:-2]):
            span = pl.ds(pl.multiple_of(owners_ref[i] * step, step), step)
            for slot in range(slots):
                at = places_ref[row * slots + slot]
                start = pl.multiple_of(jnp.maximum(at, 0) * width, width)
                part = line_ref[0, :, :, pl.ds(start, width)].reshape(step, width)
                high, low = split(jnp.where(at < 0, 0.0, part))
                high_ref[span, slot * width : (slot + 1) * width] = high
                low_ref[span, slot * width : (slot + 1) * width] = low

    shape = jax.ShapeDtypeStruct((count * height, slots * width), jnp.bfloat16)
    return pl.pallas_call(
        kernel,
        grid_spec=pltpu.PrefetchScalarGridSpec(
            num_scalar_prefetch=3,
            grid=(count,),
            in_specs=[
                pl.BlockSpec(
                    (1, groups, times, depth), lambda i, owners, blocks, places: (blocks[i], 0, 0, 0)
                )
                for _ in lines
            ],
            out_specs=[
                pl.BlockSpec((height, slots * width), lambda i, owners, blocks, places: (i, 0))
            ]
            * 2,
        ),
        out_shape=[shape, shape],
        cost_estimate=pl.CostEstimate(flops=0, bytes_accessed=0, transcendentals=0),
    )(owners, blocks, places.reshape(-1), *lines)


def product(rows, pieces, modes, heights):
    depth = rows[0].shape[1]
    height = sum(heights)
    block = math.gcd(BLOCK, modes // 2, *(start for _, start in pieces))
    steps = modes // block
    widths = [len(arrays) for arrays, _ in pieces]
    operands, in_specs = [], []
    for arrays, start in pieces:
        first, size = start // block, steps // len(arrays)
        for j, x in enumerate(arrays):
            operands.append(x)
            in_specs.append(
                pl.BlockSpec(
                    (block, x.shape[1]),
                    lambda i, first=first, size=size, j=j: (
                        first + jnp.clip(i - j * size, 0, size - 1),
                        0,
                    ),
                )
            )
    count = len(operands)

    def kernel(high_ref, low_ref, *refs):
        parts, first = [], 0
        for size in widths:
            part = refs[first][...]
            if size == 2:
                early = pl.program_id(0) < steps // 2
                part = jnp.where(early, part, refs[first + 1][...])
            parts.append(part)
            first += size
        high, low = split(parts[0] if len(parts) == 1 else jnp.concatenate(parts, axis=1))
        at = 0
        for out_ref in refs[count:]:
            span = pl.ds(at, out_ref.shape[0])
            row_high = high_ref[span, :]
            out_ref[...] = dot(row_high, high) + (dot(row_high, low) + dot(low_ref[span, :], high))
            at += out_ref.shape[0]

    return pl.pallas_call(
        kernel,
        grid=(modes // block,),
        in_specs=[pl.BlockSpec((height, depth), lambda i: (0, 0))] * 2 + in_specs,
        out_specs=[pl.BlockSpec((h, block), lambda i: (0, i)) for h in heights],
        out_shape=[jax.ShapeDtypeStruct((h, modes), jnp.float32) for h in heights],
        compiler_params=pltpu.CompilerParams(vmem_limit_bytes=48 * 2**20),
        cost_estimate=pl.CostEstimate(flops=0, bytes_accessed=0, transcendentals=0),
    )(*rows, *operands)


def put(out, parts, start, modes):
    height, span = parts[0].shape
    block = math.gcd(math.gcd(4 * BLOCK, span), start or span)
    first = start // block
    count = len(parts)

    def kernel(*refs):
        value = refs[0][...]
        for ref in refs[1:count]:
            value = value + ref[...]
        refs[-1][...] = value

    operands = list(parts)
    in_specs = [pl.BlockSpec((height, block), lambda i: (0, i)) for _ in parts]
    if out is not None:
        operands.append(out)
        in_specs.append(pl.BlockSpec(memory_space=pltpu.HBM))
    return pl.pallas_call(
        kernel,
        grid=(span // block,),
        in_specs=in_specs,
        out_specs=pl.BlockSpec((height, block), lambda i: (0, first + i)),
        out_shape=jax.ShapeDtypeStruct((height, modes), jnp.float32),
        input_output_aliases={} if out is None else {count: 0},
        compiler_params=pltpu.CompilerParams(vmem_limit_bytes=48 * 2**20),
        cost_estimate=pl.CostEstimate(flops=0, bytes_accessed=0, transcendentals=0),
    )(*operands)


def shards(snapshots, operator):
    chips = lax.axis_size("col") // CORES
    half = chips // 2
    modes, width = operator.shape
    col = lax.axis_index("col")
    chip, core = lax.div(col, CORES), lax.rem(col, CORES)
    side = (chip >= half).astype(jnp.int32)
    place = jnp.where(side == 0, half - 1 - chip, chip - half)

    def at(side, place):
        return (half - 1 - place) + side * (2 * place + 1)

    def move(x, routes, cross=0):
        pairs = [
            (at(a, i) * CORES + c, at(b, j) * CORES + (c + cross) % CORES)
            for (a, i), (b, j) in routes
            for c in range(CORES)
        ]
        return lax.ppermute(x, "col", pairs)

    def inward(x, i):
        return move(x, [((s, i), (s, 0)) for s in range(2)])

    def outward(x, i, cross=0):
        return move(x, [((s, 0), (s, i)) for s in range(2)], cross)

    def across(x, i=0, cross=0):
        return move(x, [((s, 0), (1 - s, i)) for s in range(2)], cross)

    def far(x, i):
        return move(x, [((s, i), (1 - s, 0)) for s in range(2)])

    def turn(x, i):
        return move(x, [((s, j), (s, (j + i) % half)) for s in range(2) for j in range(half)])

    def swap(x):
        return move(x, [((s, j), (s, j)) for s in range(2) for j in range(half)], 1)

    edges = [0]
    for part in SIXTEENTHS:
        edges.append(edges[-1] + modes * part // sum(SIXTEENTHS))
    count = len(SIXTEENTHS)
    spokes = range(1, half)
    chunk = [operator[edges[k] : edges[k + 1]] for k in range(2)]

    def pair(x, cut=False):
        if width % 128 == 0:
            middle = x.shape[0] // 2
            ends = (x[:middle], x[middle:]) if cut else (x,)
            return [((x,), 0), (tuple(swap(end) for end in ends), 0)]
        other = swap(x)
        ends = jnp.where(core == 0, x, other), jnp.where(core == 0, other, x)
        return [((jnp.concatenate(ends, axis=1),), 0)]

    def places_of(chips):
        if width % 128 == 0:
            return [q * CORES + e if q is not None else -1 for q in chips for e in (core, 1 - core)]
        return [-1 if q is None else q for q in chips]

    hub = across(chunk[0])
    first = [turn(chunk[1], i) for i in spokes]
    near = [snapshots] + [turn(snapshots, i) for i in reversed(spokes)]
    line = jnp.stack(near + [across(snapshots)] + [far(snapshots, i) for i in spokes])
    outer = [far(after(chunk[0], line), i) for i in spokes]
    rest = after(operator, hub)
    chunk += [rest[edges[k] : edges[k + 1]] for k in range(2, count)]
    turns = lax.axis_size("row")
    line_row = lax.axis_index("row")
    groups, times, _ = snapshots.shape
    lines = [line]
    for i in range(1, turns):
        lines.append(lax.ppermute(line, "row", [(r, (r + i) % turns) for r in range(turns)]))
    height = turns * groups * times

    def left_side(row_chips, places):
        rows = jnp.array(row_chips, jnp.int32)
        places = [places_of(chips) for chips in places]
        places = jnp.array([[jnp.asarray(x, jnp.int32) for x in row] for row in places])
        step = width if width % 128 == 0 else CORES * width
        owners = jnp.stack([lax.rem(line_row - i + turns, turns) for i in range(turns)])
        return arrange(lines, owners.astype(jnp.int32), rows, places, step)

    mine = [at(side, lax.rem(place + i, half)) for i in range(half)]
    others = [at(1 - side, i) for i in range(half)]
    columns = [at(side, lax.rem(place - i + half, half)) for i in range(half)]
    rows_a = left_side(
        range(half),
        [
            [None if i and i == j else q for j, q in enumerate(mine + others)]
            for i in range(half)
        ],
    )
    rows_b = left_side([0, *range(half, 2 * half)], [columns] * (1 + half))

    ready, totals, turned, lane = (hub,), [None], first, ()
    for k in range(1, count):
        if k == 2:
            turned = [turn(after(chunk[k], *outer, sums[0]), i) for i in spokes]
            inner = [inward(after(chunk[0], *turned), i) for i in spokes]
        elif k > 2:
            turned = [turn(after(chunk[k], *inner), i) for i in spokes]
        pieces = pair(after(chunk[k], *ready) if k == 1 else chunk[k])
        pieces += [y for x in turned for y in pair(after(x, *ready), k > 1)]
        sums = product(rows_b, pieces, edges[k + 1] - edges[k], [height] * (1 + half))
        sent = [None] * half
        for i in reversed(range(half)) if k == count - 1 else range(half):
            sent[i] = across(after(sums[1 + i], *lane), i)
        lane = sent[-1:] if k < count - 1 else ()
        totals.append([sums[0], *sent])
        ready = (sums[0], sent[0])

    pieces = [y for x in [chunk[0], *inner, hub, *outer] for y in pair(after(x, sums[0]))]
    sums = product(rows_a, pieces, edges[1], [height] * half)
    totals[0] = [sums[0]] + [outward(sums[i], i) for i in spokes]

    out = None
    for k in [*range(1, count - 1), 0, count - 1]:
        out = put(out, totals[k], edges[k], modes)
    return out.reshape(turns * groups, times, modes)


def solution(mesh):
    placed = (P("row", "col", None), P("row", "col"))
    return jax.shard_map(
        shards, mesh=mesh, in_specs=placed, out_specs=P(None, "col", "row"), check_vma=False
    )
```
